1024 devices in a mesh: expert: 64 (over x, y_lo, core), section: 8 (over z), tensor: 2 (over y_hi).
Axes of the slice: x: 8, y: 8 (y_hi: 2, y_lo: 4; y = y_hi * 4 + y_lo), z: 8, core: 2. Of those that a mesh axis runs over, the one named last changes fastest.
Arguments:
- tokens: bfloat16 [2048, 7168], P(('expert', 'tensor')), may hold values from -6 to 6
- norm_gain: float32 [7168], replicated, may hold values from 0.1 to 1.9
- expert_ids: int32 [2048, 8], P(('expert', 'tensor')), may hold values from 0 to 63, all different within a row; in each aligned block of 16 rows (0 to 15, 16 to 31, ...) at most 3 rows name the same one
- route_weights: float32 [2048, 8], P(('expert', 'tensor')), may hold values from 0.05 to 1
- gate_weight: bfloat16 [64, 7168, 1024], P('expert', 'tensor', 'section'), may hold values from -0.0625 to 0.0625
- up_weight: bfloat16 [64, 7168, 1024], P('expert', 'tensor', 'section'), may hold values from -0.0625 to 0.0625
- down_weight: bfloat16 [64, 7168, 1024], P('expert', 'tensor', 'section'), may hold values from -0.1875 to 0.1875
- queries: bfloat16 [1024, 128, 576], P(('expert', 'tensor'), 'section'), may hold values from -300 to 300
- kv_cache: bfloat16 [1024, 384, 576], P(('expert', 'tensor')), may hold values from -8 to 8
- cache_lengths: int32 [1024], P(('expert', 'tensor')), may hold values from 2 to 384
Outputs:
- moe_out: bfloat16 [2048, 7168], P(('expert', 'tensor'), 'section')
- attn_out: bfloat16 [1024, 128, 512], P(('expert', 'tensor'), 'section')
The draws below stay inside these ranges and needn't reach their ends.
Inputs may be any that keep to these rules, and one draw needn't show every extreme that they name: `expert_ids`: each row names 8 different experts; among the 16 rows of one device no expert is named more than 3 times, and on some device some expert is named exactly 3 times.
All inputs are finite; a program needn't handle non-finite values.
Results may differ from the reference program's by a relative error of at most 0.006.
Values may be sent and summed in bfloat16 or wider, within the bound.
No kernel may reach another device: no remote copies, remote signals or barrier semaphores. Data moves between devices by JAX's collectives and lax.ppermute only.
A program may use at most 64 MiB of HBM per device.

```python
import math
import jax
import jax.numpy as jnp
import numpy as np
from jax import lax

D = 7168
FF = 1024
HEADS = 128
LAT = 512
ROPE = 64
ROWS_DEV = 16
CACHE_LEN = 384
EXPERTS = 64
TOP = 8
CAP = 3
ROWS = 2048
ATT_ROWS = 1024
N_EXPERT = 64
N_TENSOR = 2


def cache_values(key):
    values = jax.random.normal(jax.random.fold_in(key, 101), (ATT_ROWS, CACHE_LEN, LAT + ROPE), jnp.float32)
    values = jnp.clip(values, -6.0, 6.0)
    return values


def draw_kv_cache(key, part):
    return cache_values(key).astype(jnp.bfloat16)


def draw_queries(key, part):
    values = jax.random.normal(jax.random.fold_in(key, 202), (ATT_ROWS, HEADS, LAT + ROPE), jnp.float32)
    values = jnp.clip(values, -6.0, 6.0)
    values = jnp.clip(values, -300.0, 300.0)
    return values.astype(jnp.bfloat16)


def place_ends(values, rng, smallest, top_value):
    longest = values.shape.index(max(values.shape))
    spots = []
    for shift in (0, 1):
        where = [jax.random.randint(jax.random.fold_in(rng, axis), (), 0, length) for axis, length in enumerate(values.shape)]
        where[longest] = (where[longest] + shift) % values.shape[longest]
        spots.append(tuple(where))
    return values.at[spots[0]].set(smallest).at[spots[1]].set(top_value)


def levels(own_key, shape, pieces, smallest, top_value):
    level = 1.0
    for position, blocks in pieces:
        steps = jax.random.uniform(jax.random.fold_in(jax.random.fold_in(own_key, 6), position), (blocks,), jnp.float32, smallest / len(pieces), top_value / len(pieces))
        level = level * jnp.repeat(jnp.exp(steps), shape[position] // blocks).reshape((-1,) + (1,) * (len(shape) - 1 - position))
    return level


def deal_out(key, own, number, rows, count, top, most, lean):
    order = jax.random.permutation(key, count)
    heavy_load, ordinary = load_shares(count, rows * top, most, lean, True), load_shares(count, rows * top, most, lean, False)
    places = jnp.arange(count)

    def named(tallies, offset_by):
        used = int((tallies > 0).sum())
        fixed = max(1, used // 4)
        passed = fixed + (places - fixed + offset_by * (used - fixed)) % max(1, count - fixed)
        return jnp.zeros((count,), jnp.int32).at[order[jnp.where(places < fixed, places, passed)]].set(jnp.asarray(tallies, jnp.int32))

    tallies = jnp.where(number % 4 == 0, named(heavy_load, number // 4), named(ordinary, number - number // 4 - 1))
    mixed = jax.random.permutation(jax.random.fold_in(own, 3), count)
    giver, taker = mixed[0:count // 2 * 2:2], mixed[1:count // 2 * 2:2]
    slack = jnp.minimum(tallies[giver] - 1, most - tallies[taker]) // 2
    slack = jnp.where((giver == order[0]) | (taker == order[0]) | (tallies[taker] == 0), 0, jnp.maximum(slack, 0))
    passed = jax.random.randint(jax.random.fold_in(own, 4), (count // 2,), 0, 1 << 20) % (slack + 1)
    tallies = tallies.at[giver].add(-passed).at[taker].add(passed)
    labels = jnp.searchsorted(jnp.cumsum(tallies), jnp.arange(rows * top), side="right").astype(jnp.int32)
    table = labels.reshape(top, rows).T
    table = table[jax.random.permutation(jax.random.fold_in(own, 1), rows)]
    offset_by = jax.random.randint(jax.random.fold_in(own, 2), (rows, 1), 0, top)
    return jnp.take_along_axis(table, (jnp.arange(top)[None, :] + offset_by) % top, axis=1)


def load_shares(amount, total, most, skew, full):
    weights = [(1 << 20) // math.isqrt(standing ** skew) + 1 for standing in range(1, amount + 1)]
    largest = most if full else min(most, max(-(-total // amount), total * weights[0] // sum(weights)))
    least = 1 if total - largest >= amount - 1 else 0
    holding, surplus = [largest] + [least] * (amount - 1), total - largest - least * (amount - 1)
    while surplus > 0:
        candidates = [i for i in range(1, amount) if holding[i] < largest] or [i for i in range(1, amount) if holding[i] < most]
        pool, left = sum([weights[i] for i in candidates]), surplus
        for i in candidates:
            more = min(most - holding[i], max(1, left * weights[i] // pool), surplus)
            holding[i] = holding[i] + more
            surplus = surplus - more
    return np.array(holding)


def gaussian(rng, dims, spread, limit, pieces=(), held_as=jnp.bfloat16):
    entries = spread * jax.random.normal(rng, dims, jnp.float32)
    if pieces:
        entries = entries * levels(rng, dims, pieces, -0.22, 0.18)
    return jnp.clip(entries, -limit, limit).astype(held_as)


def setup_inputs(seed: int = 0) -> dict:
    arg_keys = jax.random.split(jax.random.key(seed), 11)
    tokens = gaussian(arg_keys[0], (ROWS, D), 1.0, 6.0, ((0, 128),))
    norm_gain = jnp.clip(1.0 + 0.18 * jax.random.normal(arg_keys[1], (D,), jnp.float32), 0.1, 1.9)
    expert_ids_keys = jax.random.split(jax.random.fold_in(arg_keys[2], 1), ROWS // ROWS_DEV)
    expert_ids_turns = jax.random.permutation(jax.random.fold_in(arg_keys[2], 3), ROWS // ROWS_DEV)
    expert_ids = jax.vmap(lambda own, number: deal_out(jax.random.fold_in(arg_keys[2], 2), own, number, ROWS_DEV, EXPERTS, TOP, CAP, 1))(expert_ids_keys, expert_ids_turns).reshape((ROWS, TOP))
    route_weights = jnp.clip(jnp.exp(math.log(1.0) - 2.9957323 * jax.random.uniform(arg_keys[3], (ROWS, TOP), jnp.float32) ** levels(arg_keys[3], (ROWS, TOP), ((0, 128),), -0.2, 0.2)), 0.05, 1.0)
    gate_weight = gaussian(arg_keys[4], (EXPERTS, D, FF), D ** -0.5, 0.0625, ((0, 64), (1, 2), (2, 8)))
    up_weight = gaussian(arg_keys[5], (EXPERTS, D, FF), D ** -0.5, 0.0625, ((0, 64), (1, 2), (2, 8)))
    down_weight = gaussian(arg_keys[6], (EXPERTS, D, FF), FF ** -0.5, 0.1875, ((0, 64), (1, 2), (2, 8)))
    queries = draw_queries(jax.random.fold_in(arg_keys[10], 71), 0)
    kv_cache = draw_kv_cache(jax.random.fold_in(arg_keys[10], 71), 0)
    cache_lengths = place_ends(jax.random.randint(arg_keys[9], (ATT_ROWS,), 2, CACHE_LEN + 1), jax.random.fold_in(arg_keys[9], 1), 2, CACHE_LEN).astype(jnp.int32)
    return {"tokens": tokens, "norm_gain": norm_gain, "expert_ids": expert_ids, "route_weights": route_weights, "gate_weight": gate_weight, "up_weight": up_weight, "down_weight": down_weight, "queries": queries, "kv_cache": kv_cache, "cache_lengths": cache_lengths}


norm_eps = 1e-06
score_scale = 192.0 ** (-0.5)

def rms_rows(tokens, norm_gain):
    values = tokens.astype(jnp.float32)
    factor = lax.rsqrt(lax.optimization_barrier(jnp.mean(values * values, axis=-1, keepdims=True)) + norm_eps)
    return (values * factor * norm_gain).astype(jnp.bfloat16)

def attend_row(inputs):
    query_row, cache_row, length_row = inputs
    scores = jnp.dot(query_row, cache_row.T, preferred_element_type=jnp.float32) * score_scale
    is_live = jnp.arange(cache_row.shape[0], dtype=jnp.int32)[None, :] < length_row
    scores = jnp.where(is_live, scores, -jnp.inf)
    top_score = lax.optimization_barrier(jnp.max(scores, axis=-1, keepdims=True))
    powers = jnp.exp(scores - top_score)
    weights = (powers / lax.optimization_barrier(jnp.sum(powers, axis=-1, keepdims=True))).astype(jnp.bfloat16)
    return jnp.dot(weights, cache_row[:, :LAT], preferred_element_type=jnp.float32).astype(jnp.bfloat16)

def reference(tokens, norm_gain, expert_ids, route_weights, gate_weight, up_weight, down_weight, queries, kv_cache, cache_lengths):
    normed = rms_rows(tokens, norm_gain)
    slot_total = CAP * N_EXPERT * N_TENSOR

    def per_expert(running, expert):
        hits = expert_ids == expert
        weight_row = lax.optimization_barrier(jnp.sum(jnp.where(hits, route_weights, 0.0), axis=1))
        chosen = jnp.any(hits, axis=1)
        picked = jnp.nonzero(chosen, size=slot_total, fill_value=0)[0].astype(jnp.int32)
        valid = (jnp.arange(slot_total, dtype=jnp.int32) < jnp.sum(chosen.astype(jnp.int32))).astype(jnp.float32)
        inputs = normed[picked]
        gate_mat = lax.dynamic_index_in_dim(gate_weight, expert, 0, keepdims=False)
        up_mat = lax.dynamic_index_in_dim(up_weight, expert, 0, keepdims=False)
        down_mat = lax.dynamic_index_in_dim(down_weight, expert, 0, keepdims=False)
        gate = jnp.dot(inputs, gate_mat, preferred_element_type=jnp.float32)
        upper = jnp.dot(inputs, up_mat, preferred_element_type=jnp.float32)
        hidden = (jax.nn.silu(gate) * upper).astype(jnp.bfloat16)
        output = jnp.dot(hidden, down_mat.T, preferred_element_type=jnp.float32).astype(jnp.bfloat16)
        scaled = output.astype(jnp.float32) * (weight_row[picked] * valid)[:, None]
        return (running.at[picked].add(scaled), None)
    zero_sums = jnp.zeros((tokens.shape[0], tokens.shape[1]), jnp.float32)
    running, _ = lax.scan(per_expert, zero_sums, jnp.arange(EXPERTS, dtype=jnp.int32))
    moe_out = (tokens.astype(jnp.float32) + running).astype(jnp.bfloat16)
    attn_out = lax.map(attend_row, (queries, kv_cache, cache_lengths))
    return (moe_out, attn_out)
```

```python
import jax
import jax.numpy as jnp
from jax import lax
from jax.sharding import Mesh
from jax.sharding import PartitionSpec as P

LAT = 512
CAP = 3
EXPERT = ("expert_0", "expert_1", "expert_2")
EXPERT_TENSOR = ("expert_0", "expert_1", "expert_2", "tensor")


norm_eps = 1e-06
score_scale = 192.0 ** (-0.5)


def rms_rows(tokens, norm_gain):
    values = tokens.astype(jnp.float32)
    factor = lax.rsqrt(jnp.mean(values * values, axis=-1, keepdims=True) + norm_eps)
    return (values * factor * norm_gain).astype(jnp.bfloat16)


def attend(queries, kv_cache, cache_lengths):
    scores = (
        jnp.einsum("rhc,rlc->rhl", queries, kv_cache, preferred_element_type=jnp.float32)
        * score_scale
    )
    position = jnp.arange(kv_cache.shape[1], dtype=jnp.int32)
    is_live = position[None, None, :] < cache_lengths[:, None, None]
    scores = jnp.where(is_live, scores, -jnp.inf)
    top_score = jnp.max(scores, axis=-1, keepdims=True)
    powers = jnp.exp(scores - top_score)
    weights = (powers / jnp.sum(powers, axis=-1, keepdims=True)).astype(jnp.bfloat16)
    latents = kv_cache[:, :, :LAT]
    return jnp.einsum("rhl,rlc->rhc", weights, latents, preferred_element_type=jnp.float32).astype(
        jnp.bfloat16
    )


def swapped(value, axis, by):
    size = lax.axis_size(axis)
    return lax.ppermute(value, axis, [(i, i ^ by) for i in range(size)])


def per_device(
    tokens,
    norm_gain,
    expert_ids,
    route_weights,
    gate_weight,
    up_weight,
    down_weight,
    queries,
    kv_cache,
    cache_lengths,
):
    f32, bf16 = jnp.float32, jnp.bfloat16
    experts = lax.axis_size(EXPERT)
    sections = lax.axis_size("section")
    tensors = lax.axis_size("tensor")
    section = lax.axis_index("section")
    parity = section % 2
    upper = section // (sections // 2)
    rows, width = tokens.shape
    half, units = gate_weight.shape[1:]
    quarter = half // 2
    eighth = quarter // 2
    piece = half // sections

    halves = jnp.stack([gate_weight[0], up_weight[0]]).reshape(2, 2, quarter, units)
    kept = lax.dynamic_index_in_dim(halves, parity, 1, keepdims=False)
    given = lax.dynamic_index_in_dim(halves, 1 - parity, 1, keepdims=False)
    taken = swapped(given, "section", 1)
    down_parts = jnp.moveaxis(down_weight[0].reshape(sections // 2, 2, piece, units), 1, 0)
    down_cols = lax.all_to_all(
        down_parts.reshape(sections, piece, units), "section", 0, 0, tiled=True
    )

    normed = rms_rows(tokens, norm_gain)
    slot_count = experts * CAP
    choose = (expert_ids[:, :, None] == jnp.arange(experts, dtype=jnp.int32)).astype(f32)
    per_row = jnp.sum(choose, axis=1)
    before = (jnp.arange(rows)[:, None] > jnp.arange(rows)[None, :]).astype(f32)
    earlier = jnp.dot(before, per_row)
    slots = jnp.arange(slot_count, dtype=jnp.int32)
    ranking = jnp.sum(choose * earlier[:, None, :], axis=2).astype(jnp.int32)
    slot_of = expert_ids * CAP + ranking
    matches = slot_of[:, :, None] == slots
    placing = jnp.sum(matches.astype(f32), axis=1).astype(bf16)
    mixing = jnp.sum(jnp.where(matches, route_weights[:, :, None], 0.0), axis=1)
    own = lax.dynamic_index_in_dim(
        normed.reshape(rows, tensors, 2, quarter), parity, 2, keepdims=False
    )
    packed = lax.dot_general(
        placing, own.reshape(rows, tensors * quarter), (((0,), (0,)), ((), ())),
        preferred_element_type=f32,
    ).astype(bf16)
    packed = packed.reshape(experts, CAP, tensors, 2, eighth).transpose(0, 2, 3, 1, 4)
    arrived = lax.all_to_all(
        packed.reshape(experts * tensors, 2, CAP * eighth), EXPERT_TENSOR, 0, 0, tiled=True
    )
    sources = experts * tensors
    inputs = arrived.reshape(sources, 2, CAP, eighth).transpose(0, 2, 1, 3)
    inputs = inputs.reshape(sources * CAP, quarter)

    def partial(weights):
        both = jnp.concatenate([weights[0], weights[1]], axis=1)
        return jnp.dot(inputs, both, preferred_element_type=f32)

    theirs = partial(taken).astype(bf16)
    sums = partial(kept) + swapped(theirs, "section", 1).astype(f32)
    sums = sums + swapped(sums.astype(bf16), "tensor", 1).astype(f32)
    hidden = (jax.nn.silu(sums[:, :units]) * sums[:, units:]).astype(bf16)

    copies = jnp.broadcast_to(hidden, (sections, *hidden.shape))
    hidden_all = lax.all_to_all(copies, "section", 0, 0, tiled=True)
    expert_out = lax.dot_general(
        jnp.moveaxis(hidden_all, 0, 1).reshape(sources * CAP, sections * units),
        jnp.moveaxis(down_cols, 0, 1).reshape(piece, sections * units),
        (((1,), (1,)), ((), ())),
        preferred_element_type=f32,
    ).astype(bf16)
    returned = lax.all_to_all(
        expert_out.reshape(sources, CAP, piece), EXPERT_TENSOR, 0, 0, tiled=True
    )
    returned = returned.reshape(experts, tensors, CAP, piece).transpose(1, 0, 2, 3)
    returned = returned.reshape(tensors, slot_count, piece)
    mixed = jnp.einsum("rs,tsc->trc", mixing, returned.astype(f32))
    mine = lax.dynamic_index_in_dim(mixed, upper, 0, keepdims=False)
    other = lax.dynamic_index_in_dim(mixed, 1 - upper, 0, keepdims=False)
    got = swapped(other, "section", sections // 2)
    summed = jnp.where(
        upper == 0, jnp.concatenate([mine, got], axis=1), jnp.concatenate([got, mine], axis=1)
    )
    own_width = width // sections
    own_cols = lax.dynamic_slice_in_dim(tokens, section * own_width, own_width, 1)
    moe_out = (own_cols.astype(f32) + summed).astype(bf16)
    attn_out = attend(queries, kv_cache, cache_lengths)
    return (moe_out, attn_out)


def solution(mesh):
    experts = mesh.shape["expert"]
    torus = Mesh(
        mesh.devices.reshape(experts // 8, 4, 2, mesh.shape["section"], mesh.shape["tensor"]),
        ("expert_0", "expert_1", "expert_2", "section", "tensor"),
    )
    return jax.shard_map(
        per_device,
        mesh=torus,
        in_specs=(
            P(EXPERT_TENSOR, None),
            P(),
            P(EXPERT_TENSOR, None),
            P(EXPERT_TENSOR, None),
            P(EXPERT, "tensor", "section"),
            P(EXPERT, "tensor", "section"),
            P(EXPERT, "tensor", "section"),
            P(EXPERT_TENSOR, "section", None),
            P(EXPERT_TENSOR, None, None),
            P(EXPERT_TENSOR),
        ),
        out_specs=(P(EXPERT_TENSOR, "section"), P(EXPERT_TENSOR, "section", None)),
        check_vma=False,
    )
```
